32 devices in a mesh: dp: 16 (over z, y, core), tensor: 2 (over x).
Axes of the slice: x: 2, y: 2, z: 4, core: 2. Of those that a mesh axis runs over, the one named last changes fastest.
Arguments:
- tokens: bfloat16 [8192, 1024], P(('dp', 'tensor')), may hold values from -6 to 6
- teacher: bfloat16 [8192, 1024], P(('dp', 'tensor')), may hold values from -6 to 6
- segment_ids: int32 [8192], P('dp'), may hold values from 0 to 8191, as said below
- variate_ids: int32 [8192], P('dp'), may hold values from 0 to 8191, as said below
- time_ids: int32 [8192], P('dp'), may hold values from 0 to 127, as said below
- valid: int32 [8192], P('dp'), may hold values from 0 to 1
- w_query: bfloat16 [1024, 1024], P('dp', 'tensor'), may hold values from -0.1875 to 0.1875
- w_key: bfloat16 [1024, 1024], P('dp', 'tensor'), may hold values from -0.1875 to 0.1875
- w_value: bfloat16 [1024, 1024], P('dp', 'tensor'), may hold values from -0.1875 to 0.1875
- w_out: bfloat16 [1024, 1024], P('tensor', 'dp'), may hold values from -0.75 to 0.75
- w_gate: bfloat16 [1024, 4096], P('dp', 'tensor'), may hold values from -0.1875 to 0.1875
- w_up: bfloat16 [1024, 4096], P('dp', 'tensor'), may hold values from -0.1875 to 0.1875
- w_down: bfloat16 [4096, 1024], P('tensor', 'dp'), may hold values from -0.1875 to 0.1875
- gain_attn: bfloat16 [1024], P('dp'), may hold values from 0.25 to 1.75
- gain_ffn: bfloat16 [1024], P('dp'), may hold values from 0.25 to 1.75
- attn_bias: float32 [2, 16], P(None, 'tensor'), may hold values from -1.5 to 1.5
Outputs:
- mixed: bfloat16 [8192, 1024], P(('dp', 'tensor'))
- loss: float32 [], replicated
- grad_tokens: float32 [8192, 1024], P(('dp', 'tensor'))
- grad_query: float32 [1024, 1024], P('dp', 'tensor')
- grad_key: float32 [1024, 1024], P('dp', 'tensor')
- grad_value: float32 [1024, 1024], P('dp', 'tensor')
- grad_out: float32 [1024, 1024], P('tensor', 'dp')
- grad_gate: float32 [1024, 4096], P('dp', 'tensor')
- grad_up: float32 [1024, 4096], P('dp', 'tensor')
- grad_down: float32 [4096, 1024], P('tensor', 'dp')
- grad_gain_attn: float32 [1024], P('dp')
- grad_gain_ffn: float32 [1024], P('dp')
- grad_attn_bias: float32 [2, 16], P(None, 'tensor')
The draws below stay inside these ranges and needn't reach their ends.
Inputs may be any that keep to these rules, and one draw needn't show every extreme that they name: `segment_ids`: A token's id is the index, in the whole array, of its document's first token; within a sequence of 512 tokens the ids never fall, and every sequence's first token begins a new id; documents differ widely in length. `variate_ids`: A token's id is the index, in the whole array, of the first token of its run; the ids never fall within a sequence and change wherever segment_ids changes, and also inside documents. `time_ids`: each token's position counted from the last change of variate_ids, 0 at that change.
All inputs are finite; a program needn't handle non-finite values.
Results may differ from the reference program's by a relative error of at most 0.017.
Values may be sent and summed in bfloat16 or wider, within the bound.
No kernel may reach another device: no remote copies, remote signals or barrier semaphores. Data moves between devices by JAX's collectives and lax.ppermute only.
A program may use at most 128 MiB of HBM per device.

```python
import jax
import jax.numpy as jnp
from jax import lax

HEADS = 16
HEAD_DIM = 64
FF = 4096
D = 1024
SEQ_LEN = 512
TOKENS = 8192


def layout_ids(key):
    positions = jnp.arange(TOKENS, dtype=jnp.int32)
    in_sequence = positions % SEQ_LEN
    period = min(128, SEQ_LEN // 4)
    run_rate = min(96, max(SEQ_LEN // 8, 2))
    rate_key, doc_key, run_key = jax.random.split(jax.random.fold_in(key, 17), 3)
    groups = (TOKENS + 63) // 64
    levels = jax.random.randint(rate_key, (groups,), 0, 4)
    spacing = jnp.array([24, 96, 768, 6144], dtype=jnp.int32)
    level_rows = jnp.repeat(levels, 64, total_repeat_length=groups * 64)[:TOKENS]
    spacing_rows = jnp.take(spacing, level_rows)
    quiet = positions < period
    random_doc = (jax.random.randint(doc_key, (TOKENS,), 0, spacing_rows) == 0) & jnp.logical_not(quiet)
    doc_start = random_doc | (in_sequence == 0) | (positions == TOKENS - 1)
    random_run = (jax.random.randint(run_key, (TOKENS,), 0, run_rate) == 0) & jnp.logical_not(quiet)
    run_start = doc_start | random_run | (in_sequence % period == 0)
    doc_anchor = lax.cummax(jnp.where(doc_start, positions, 0), axis=0)
    run_anchor = lax.cummax(jnp.where(run_start, positions, 0), axis=0)
    return (doc_anchor.astype(jnp.int32), run_anchor.astype(jnp.int32), (positions - run_anchor).astype(jnp.int32))


def draw_segment_ids(key, part):
    return layout_ids(key)[0]


def draw_variate_ids(key, part):
    return layout_ids(key)[1]


def draw_time_ids(key, part):
    return layout_ids(key)[2]


def draw_valid(key, part):
    positions = jnp.arange(TOKENS, dtype=jnp.int32)
    picks = jax.random.randint(jax.random.fold_in(key, 29), (TOKENS,), 0, 4 * TOKENS)
    return (picks < TOKENS + 2 * positions).astype(jnp.int32)


def steps_of(key, dims, shards, smallest, top_value):
    loudness = 1.0
    for position, shards_of in shards:
        draws = jax.random.uniform(jax.random.fold_in(jax.random.fold_in(key, 6), position), (shards_of,), jnp.float32, smallest / len(shards), top_value / len(shards))
        loudness = loudness * jnp.repeat(jnp.exp(draws), dims[position] // shards_of).reshape((-1,) + (1,) * (len(dims) - 1 - position))
    return loudness


def gaussian(rng, shape, deviation, bound, cuts=(), held_as=jnp.bfloat16):
    values = deviation * jax.random.normal(rng, shape, jnp.float32)
    if cuts:
        values = values * steps_of(rng, shape, cuts, -0.22, 0.18)
    return jnp.clip(values, -bound, bound).astype(held_as)


def setup_inputs(seed: int = 0) -> dict:
    keys = jax.random.split(jax.random.key(seed), 17)
    return {
        "tokens": gaussian(keys[0], (TOKENS, D), 1.0, 6.0, ((0, 32),)),
        "teacher": gaussian(keys[1], (TOKENS, D), 1.0, 6.0, ((0, 32),)),
        "segment_ids": draw_segment_ids(jax.random.fold_in(keys[16], 71), 0),
        "variate_ids": draw_variate_ids(jax.random.fold_in(keys[16], 71), 0),
        "time_ids": draw_time_ids(jax.random.fold_in(keys[16], 71), 0),
        "valid": draw_valid(jax.random.fold_in(keys[16], 71), 0),
        "w_query": gaussian(keys[6], (D, D), D ** -0.5, 0.1875, ((0, 16), (1, 2))),
        "w_key": gaussian(keys[7], (D, D), D ** -0.5, 0.1875, ((0, 16), (1, 2))),
        "w_value": gaussian(keys[8], (D, D), D ** -0.5, 0.1875, ((0, 16), (1, 2))),
        "w_out": gaussian(keys[9], (D, D), (D // 16) ** -0.5, 0.75, ((0, 2), (1, 16))),
        "w_gate": gaussian(keys[10], (D, FF), D ** -0.5, 0.1875, ((0, 16), (1, 2))),
        "w_up": gaussian(keys[11], (D, FF), D ** -0.5, 0.1875, ((0, 16), (1, 2))),
        "w_down": gaussian(keys[12], (FF, D), (FF // 4) ** -0.5, 0.1875, ((0, 2), (1, 16))),
        "gain_attn": jnp.clip(1.0 + 0.15 * jax.random.normal(keys[13], (D,), jnp.float32), 0.25, 1.75).astype(jnp.bfloat16),
        "gain_ffn": jnp.clip(1.0 + 0.15 * jax.random.normal(keys[14], (D,), jnp.float32), 0.25, 1.75).astype(jnp.bfloat16),
        "attn_bias": jnp.clip(jax.random.uniform(keys[15], (2, HEADS), jnp.float32, -1.5, 1.5) * steps_of(keys[15], (2, HEADS), ((1, 2),), -0.4, 0.0), -1.5, 1.5),
    }


@jax.custom_vjp
def low(v):
    return lax.optimization_barrier(v.astype(jnp.bfloat16)).astype(jnp.float32)

@jax.custom_vjp
def low_back(v):
    return v

def low_keep(v):
    return (low(v), None)

def low_pass(kept, grad):
    return (grad,)

def back_keep(v):
    return (v, None)

def back_low(kept, grad):
    return (low(grad),)
low.defvjp(low_keep, low_pass)
low_back.defvjp(back_keep, back_low)
norm_eps = 1e-06
highest = lax.Precision.HIGHEST

def rms_norm(values_in, gain_vec):
    inv_root = lax.rsqrt(lax.optimization_barrier(jnp.mean(values_in * values_in, axis=-1, keepdims=True)) + norm_eps)
    return values_in * inv_root * gain_vec

def rotate(values_in, positions):
    half_dim = values_in.shape[-1] // 2
    frequency = 10000.0 ** (-jnp.arange(half_dim, dtype=jnp.float32) / half_dim)
    angles = positions.astype(jnp.float32)[:, None, None] * frequency
    cosines = jnp.cos(angles)
    sines = jnp.sin(angles)
    first_half = values_in[..., :half_dim]
    second_half = values_in[..., half_dim:]
    return jnp.concatenate([first_half * cosines - second_half * sines, second_half * cosines + first_half * sines], axis=-1)

def attend(queries, keys_all, values_all, segments, variates, bias_pair):
    length = queries.shape[0]
    block_rows = min(512, length)

    def one_block(block_index, queries, keys_all, values_all, segments, variates, bias_pair):
        row_start = block_index * block_rows
        query_block = lax.dynamic_slice_in_dim(queries, row_start, block_rows, 0)
        seg_block = lax.dynamic_slice_in_dim(segments, row_start, block_rows, 0)
        var_block = lax.dynamic_slice_in_dim(variates, row_start, block_rows, 0)
        same_segment = seg_block[:, None] == segments[None, :]
        same_variate = same_segment & (var_block[:, None] == variates[None, :])
        scores = jnp.einsum('qhd,khd->hqk', query_block, keys_all, precision=highest)
        scores = scores + jnp.where(same_variate[None], bias_pair[0][:, None, None], bias_pair[1][:, None, None])
        scores = low_back(scores)
        scores = jnp.where(same_segment[None], scores, -1000000000.0)
        log_total = jax.nn.logsumexp(scores, axis=-1, keepdims=True)
        weights = low(jnp.exp(scores - log_total))
        return jnp.einsum('hqk,khd->qhd', weights, values_all, precision=highest)
    checked = jax.checkpoint(one_block)
    blocks = lax.map(lambda block_index: checked(block_index, queries, keys_all, values_all, segments, variates, bias_pair), jnp.arange(length // block_rows, dtype=jnp.int32))
    return blocks.reshape(queries.shape)

def layer_rows(params, inputs, segments, variates, positions):
    w_query, w_key, w_value, w_out, w_gate, w_up, w_down, gain_one, gain_two, bias_pair = params
    length = inputs.shape[0]
    head_shape = (length, w_query.shape[1] // HEAD_DIM, HEAD_DIM)
    normed = low(rms_norm(inputs, gain_one))
    proj_query = low_back(jnp.dot(normed, w_query, precision=highest))
    proj_key = low_back(jnp.dot(normed, w_key, precision=highest))
    proj_value = low_back(jnp.dot(normed, w_value, precision=highest))
    queries = low(rotate(proj_query.reshape(head_shape), positions) * HEAD_DIM ** (-0.5))
    keys_all = low(rotate(proj_key.reshape(head_shape), positions))
    values_all = low(proj_value.reshape(head_shape))
    attended = attend(queries, keys_all, values_all, segments, variates, bias_pair)
    attn_heads = low(low_back(attended.reshape(length, -1)))
    middle = inputs + low_back(jnp.dot(attn_heads, w_out, precision=highest))
    normed_two = low(rms_norm(middle, gain_two))
    gate = low_back(jnp.dot(normed_two, w_gate, precision=highest))
    upward = low_back(jnp.dot(normed_two, w_up, precision=highest))
    hidden = low(jax.nn.silu(gate) * upward)
    return middle + low_back(jnp.dot(hidden, w_down, precision=highest))

def reference(tokens, teacher, segment_ids, variate_ids, time_ids, valid, w_query, w_key, w_value, w_out, w_gate, w_up, w_down, gain_attn, gain_ffn, attn_bias):
    params = tuple((weight.astype(jnp.float32) for weight in (w_query, w_key, w_value, w_out, w_gate, w_up, w_down, gain_attn, gain_ffn))) + (attn_bias.astype(jnp.float32),)
    seq_count = tokens.shape[0] // SEQ_LEN

    def shaped(array_in):
        return array_in.reshape((seq_count, SEQ_LEN) + array_in.shape[1:])
    inputs = shaped(tokens.astype(jnp.float32))
    targets = shaped(teacher.astype(jnp.float32))
    segments = shaped(segment_ids)
    variates = shaped(variate_ids)
    positions = shaped(time_ids)
    keeping = shaped(valid.astype(jnp.float32))
    valid_count = jnp.sum(valid.astype(jnp.float32))
    row_layer = jax.checkpoint(layer_rows)

    def objective(params, inputs):

        def one_sequence(carried, stepped):
            seq_in, seq_target, seq_seg, seq_var, seq_pos, seq_keep = stepped
            result = row_layer(params, seq_in, seq_seg, seq_var, seq_pos)
            errors = result - seq_target
            return (carried + jnp.sum(seq_keep[:, None] * errors * errors), result)
        square_total, results = lax.scan(one_sequence, jnp.zeros((), jnp.float32), (inputs, targets, segments, variates, positions, keeping))
        return (square_total * (TOKENS / (2.0 * valid_count)), (results, square_total))
    primal, backward, extras = jax.vjp(objective, params, inputs, has_aux=True)
    param_grads, input_grads = backward(jnp.ones((), jnp.float32))
    results, square_total = extras
    loss = square_total / (D * valid_count)
    return (results.reshape(TOKENS, D).astype(jnp.bfloat16), loss, input_grads.reshape(TOKENS, D), param_grads[0], param_grads[1], param_grads[2], param_grads[3], param_grads[4], param_grads[5], param_grads[6], param_grads[7], param_grads[8], param_grads[9])
```

```python
import jax
import jax.numpy as jnp
from jax import lax
from jax.sharding import PartitionSpec as P

HEAD_DIM = 64
EPS = 1e-06
BF = jnp.bfloat16
F32 = jnp.float32


def dot(left, right, cl, cr):
    return lax.dot_general(left, right, (((cl,), (cr,)), ((), ())), preferred_element_type=F32)


def rotary(positions):
    half = HEAD_DIM // 2
    frequency = 10000.0 ** (-jnp.arange(half, dtype=F32) / half)
    angles = positions.astype(F32)[:, None, None] * frequency
    return jnp.cos(angles), jnp.sin(angles)


def turn(values, cosines, sines):
    half = HEAD_DIM // 2
    first, second = values[..., :half], values[..., half:]
    return jnp.concatenate(
        [first * cosines - second * sines, second * cosines + first * sines], axis=-1
    )


class Links:
    def __init__(self, dp, tp):
        self.dp, self.tp = dp, tp
        self.inner = 4
        self.zc = dp // self.inner

    def xor(self, value, mask):
        return lax.ppermute(value, "dp", [(i, i ^ mask) for i in range(self.dp)])

    def core(self, value):
        return self.xor(value, 1)

    def y(self, value):
        return self.xor(value, 2)

    def z(self, value, step):
        shift = step * self.inner
        return lax.ppermute(value, "dp", [(i, (i + shift) % self.dp) for i in range(self.dp)])

    def x(self, value, shift):
        return lax.ppermute(
            value, "tensor", [(i, (i + shift) % self.tp) for i in range(self.tp)]
        )

    def gather(self, shard):
        line = [shard]
        for _ in range(self.zc - 1):
            line.append(self.z(line[-1], 1))
        own = jnp.concatenate(line + [self.y(block) for block in line], axis=0)
        return own, self.core(own)

    def scatter(self, own, arrived):
        total = own + arrived.astype(F32)
        quarter = total.shape[0] // 2
        away = self.y(total[quarter:].astype(BF))
        total = total[:quarter] + away.astype(F32)
        block = quarter // self.zc
        piece = total[quarter - block :]
        for k in range(self.zc - 2, -1, -1):
            moved = self.z(piece.astype(BF), -1)
            piece = total[k * block : (k + 1) * block] + moved.astype(F32)
        return piece

    def scatter_small(self, vector):
        half = vector.shape[1] // 2
        total = vector[:, :half] + self.core(vector[:, half:])
        quarter = half // 2
        total = total[:, :quarter] + self.y(total[:, quarter:])
        block = quarter // self.zc
        piece = total[:, quarter - block :]
        for k in range(self.zc - 2, -1, -1):
            piece = total[:, k * block : (k + 1) * block] + self.z(piece, -1)
        return piece

    def sum_dp(self, value):
        mask = 1
        while mask < self.dp:
            value = value + self.xor(value, mask)
            mask *= 2
        return value

    def sum_x(self, value):
        total = value
        for shift in range(1, self.tp):
            total = total + self.x(value, shift)
        return total


def local(
    tokens,
    teacher,
    segment_ids,
    variate_ids,
    time_ids,
    valid,
    w_query,
    w_key,
    w_value,
    w_out,
    w_gate,
    w_up,
    w_down,
    gain_attn,
    gain_ffn,
    attn_bias,
):
    rows, width = tokens.shape
    dp, tp = lax.axis_size("dp"), lax.axis_size("tensor")
    links = Links(dp, tp)
    zc = links.zc
    length = rows * tp
    all_tokens = dp * length
    half = width // 2
    block = width // dp
    me_x = lax.axis_index("tensor")
    me_dp = lax.axis_index("dp")
    hd = w_query.shape[1]
    heads = hd // HEAD_DIM
    ff = w_gate.shape[1]
    inv_scale = HEAD_DIM ** (-0.5)

    place = jnp.arange(width, dtype=jnp.int32)
    inner = place % block
    z_rel = (place // block) % zc
    y_rel = (place // (block * zc)) % 2
    c_rel = place // half
    my_z, my_y, my_c = me_dp // 4, (me_dp // 2) % 2, me_dp % 2
    absolute = (
        ((my_z - z_rel + zc) % zc) * 4 + (my_y ^ y_rel) * 2 + (my_c ^ c_rel)
    ) * block + inner
    chooser = (jnp.arange(width, dtype=jnp.int32)[:, None] == absolute[None, :]).astype(BF)

    valid_sum = jnp.sum(valid)
    extra = jnp.concatenate(
        [
            gain_attn[:, None],
            gain_ffn[:, None],
            jnp.broadcast_to((valid_sum // 256).astype(BF), (block, 1)),
            jnp.broadcast_to((valid_sum % 256).astype(BF), (block, 1)),
            jnp.zeros((block, 124), BF),
        ],
        axis=1,
    )
    wave_a = links.gather(
        jnp.concatenate([w_query, w_key, w_value, w_out.T, extra], axis=1)
    )
    wave_g = links.gather(jnp.concatenate([w_gate, w_up], axis=1))
    wave_d = links.gather(w_down.T)

    def columns(wave, start, size):
        return tuple(part[:, start : start + size] for part in wave)

    w_qkv = columns(wave_a, 0, 3 * hd)
    w_o = columns(wave_a, 3 * hd, hd)
    extras = columns(wave_a, 4 * hd, 128)
    picker = (
        jnp.arange(8, dtype=jnp.int32)[:, None] == jnp.arange(128, dtype=jnp.int32)[None, :]
    ).astype(BF)
    picked = jnp.concatenate([dot(picker, part, 1, 1) for part in extras], axis=1)
    gain_one, gain_two = picked[0], picked[1]
    valid_count = (jnp.sum(picked[2]) * 256.0 + jnp.sum(picked[3])) / block

    def into(acts, wave):
        return dot(acts[:, :half], wave[0], 1, 0) + dot(acts[:, half:], wave[1], 1, 0)

    def back(acts, *waves):
        sides = []
        for side in range(2):
            total = None
            for act, wave in zip(acts, waves):
                term = dot(act, wave[side], 1, 1)
                total = term if total is None else total + term
            sides.append(total)
        return jnp.concatenate(sides, axis=1)

    def share(value):
        return [value] + [links.x(value, -shift) for shift in range(1, tp)]

    def collect(partials):
        total = partials[0]
        for shift in range(1, tp):
            total = total + links.x(partials[shift].astype(BF), shift).astype(F32)
        return total

    def part(value, r):
        return value[r * rows : (r + 1) * rows]

    def relative(ids):
        return lax.dynamic_slice_in_dim(jnp.concatenate([ids, ids]), me_x * rows, length, 0)

    segments, variates, positions, keeping = (
        relative(ids) for ids in (segment_ids, variate_ids, time_ids, valid)
    )
    keep_own = keeping[:rows].astype(F32)[:, None]

    placed = dot(jnp.concatenate([tokens, teacher], axis=0), chooser, 1, 0).astype(BF)
    target = placed[rows:].astype(F32)
    x_all = jnp.concatenate(share(placed[:rows]), axis=0).astype(F32)
    root_one = lax.rsqrt(jnp.mean(x_all * x_all, axis=-1, keepdims=True) + EPS)
    unit_one = x_all * root_one
    acts = (unit_one * gain_one).astype(BF)

    qkv = into(acts, w_qkv)
    cosines, sines = rotary(positions)
    shape = (length, heads, HEAD_DIM)
    queries = (turn(qkv[:, :hd].reshape(shape), cosines, sines) * inv_scale).astype(BF)
    keys = turn(qkv[:, hd : 2 * hd].reshape(shape), cosines, sines).astype(BF)
    values = qkv[:, 2 * hd :].reshape(shape).astype(BF)

    block_rows = min(512, length)
    blocks = length // block_rows
    bias_same = attn_bias[0][:, None, None]
    bias_other = attn_bias[1][:, None, None]

    def rows_of(array, index):
        return lax.dynamic_slice_in_dim(array, index * block_rows, block_rows, 0)

    def score_block(index):
        query_block = rows_of(queries, index)
        seg_block, var_block = rows_of(segments, index), rows_of(variates, index)
        same_segment = seg_block[:, None] == segments[None, :]
        same_variate = same_segment & (var_block[:, None] == variates[None, :])
        scores = jnp.einsum("qhd,khd->hqk", query_block, keys, preferred_element_type=F32)
        scores = scores + jnp.where(same_variate[None], bias_same, bias_other)
        return jnp.where(same_segment[None], scores, -1000000000.0), query_block, same_variate

    def forward_block(index):
        scores = score_block(index)[0]
        log_total = jax.nn.logsumexp(scores, axis=-1, keepdims=True)
        probs = jnp.exp(scores - log_total).astype(BF)
        return jnp.einsum("hqk,khd->qhd", probs, values, preferred_element_type=F32), log_total

    block_ids = jnp.arange(blocks, dtype=jnp.int32)
    attended, log_totals = lax.map(forward_block, block_ids)
    attn = attended.reshape(length, hd).astype(BF)

    order = list(range(1, tp)) + [0]
    delta = {}
    for r in order:
        delta[r] = back((part(attn, r),), w_o)
    x_own = placed[:rows].astype(F32)
    middle = x_own + collect(delta)

    root_two = lax.rsqrt(jnp.mean(middle * middle, axis=-1, keepdims=True) + EPS)
    unit_two = middle * root_two
    ffn_parts = share((unit_two * gain_two).astype(BF))
    w_g, w_u = columns(wave_g, 0, ff), columns(wave_g, ff, ff)
    gates = [into(act, w_g) for act in ffn_parts]
    ups = [into(act, w_u) for act in ffn_parts]
    hiddens = [(jax.nn.silu(g) * u).astype(BF) for g, u in zip(gates, ups)]
    branch = {}
    for r in order:
        branch[r] = back((hiddens[r],), wave_d)
    result = middle + collect(branch)

    errors = result - target
    square_sum = jnp.sum(keep_own * errors * errors)
    grad_result = keep_own * errors * (all_tokens / valid_count)
    out_parts = share(grad_result.astype(BF))
    gate_grads, up_grads = [], []
    for act, g, u in zip(out_parts, gates, ups):
        grad_hidden = into(act, wave_d)
        sig = 1.0 / (1.0 + jnp.exp(-g))
        gate_grads.append((grad_hidden * u * sig * (1.0 + g * (1.0 - sig))).astype(BF))
        up_grads.append((grad_hidden * (g * sig)).astype(BF))
    ffn_back = {}
    for r in order:
        ffn_back[r] = back((gate_grads[r], up_grads[r]), w_g, w_u)
    grad_b = collect(ffn_back)

    def reduce_grad(left, right):
        arrived = links.core(dot(left[:, half:], right, 0, 0).astype(BF))
        return links.scatter(dot(left[:, :half], right, 0, 0), arrived)

    ffn_all = jnp.concatenate(ffn_parts, axis=0)
    out_all = jnp.concatenate(out_parts, axis=0)
    hidden_all = jnp.concatenate(hiddens, axis=0)
    sum_down = reduce_grad(out_all, hidden_all).T
    sum_gate = reduce_grad(ffn_all, jnp.concatenate(gate_grads, axis=0))
    sum_up = reduce_grad(ffn_all, jnp.concatenate(up_grads, axis=0))

    gain_two_part = jnp.sum(grad_b * unit_two, axis=0)
    scaled = grad_b * gain_two
    grad_middle = grad_result + root_two * (
        scaled - unit_two * jnp.mean(scaled * unit_two, axis=-1, keepdims=True)
    )
    mid_all = jnp.concatenate(share(grad_middle.astype(BF)), axis=0)
    grad_heads = into(mid_all, w_o).astype(BF).reshape(shape)

    def backward_block(carried, stepped):
        grad_keys, grad_values, grad_bias = carried
        index, log_total = stepped
        scores, query_block, same_variate = score_block(index)
        probs = jnp.exp(scores - log_total)
        probs_low = probs.astype(BF)
        grad_block = rows_of(grad_heads, index)
        grad_probs = jnp.einsum("qhd,khd->hqk", grad_block, values, preferred_element_type=F32)
        delta_rows = jnp.sum(probs * grad_probs, axis=-1, keepdims=True)
        grad_scores = (probs * (grad_probs - delta_rows)).astype(BF)
        grad_queries = jnp.einsum("hqk,khd->qhd", grad_scores, keys, preferred_element_type=F32)
        grad_keys = grad_keys + jnp.einsum(
            "hqk,qhd->khd", grad_scores, query_block, preferred_element_type=F32
        )
        grad_values = grad_values + jnp.einsum(
            "hqk,qhd->khd", probs_low, grad_block, preferred_element_type=F32
        )
        same_part = jnp.sum(
            jnp.where(same_variate[None], grad_scores, 0), axis=(1, 2), dtype=F32
        )
        whole_part = jnp.sum(grad_scores, axis=(1, 2), dtype=F32)
        grad_bias = grad_bias + jnp.stack([same_part, whole_part - same_part])
        return (grad_keys, grad_values, grad_bias), grad_queries

    start = (jnp.zeros(shape, F32), jnp.zeros(shape, F32), jnp.zeros((2, heads), F32))
    (grad_keys, grad_values, grad_bias), grad_queries = lax.scan(
        backward_block, start, (block_ids, log_totals)
    )
    grad_qkv = jnp.concatenate(
        [
            (turn(grad_queries.reshape(shape), cosines, -sines) * inv_scale)
            .astype(BF)
            .reshape(length, hd),
            turn(grad_keys, cosines, -sines).astype(BF).reshape(length, hd),
            grad_values.astype(BF).reshape(length, hd),
        ],
        axis=1,
    )

    other_low = jnp.concatenate(
        [
            dot(acts[:, half:], grad_qkv, 0, 0).astype(BF),
            dot(mid_all[:, half:], attn, 0, 0).astype(BF),
        ],
        axis=1,
    )
    arrived = links.core(other_low)
    own_part = jnp.concatenate(
        [dot(acts[:, :half], grad_qkv, 0, 0), dot(mid_all[:, :half], attn, 0, 0)], axis=1
    )
    sum_attn = links.scatter(own_part, arrived)

    grad_a_parts = {}
    for r in order:
        grad_a_parts[r] = back((part(grad_qkv, r),), w_qkv)
    grad_a = collect(grad_a_parts)
    gain_one_part = sum(
        jnp.sum(grad_a_parts[r] * part(unit_one, r), axis=0) for r in range(tp)
    )
    scaled = grad_a * gain_one
    unit_own, root_own = unit_one[:rows], root_one[:rows]
    grad_tokens = grad_middle + root_own * (
        scaled - unit_own * jnp.mean(scaled * unit_own, axis=-1, keepdims=True)
    )

    gains = links.scatter_small(links.sum_x(jnp.stack([gain_one_part, gain_two_part])))
    small = jnp.concatenate([grad_bias, jnp.full((2, 1), links.sum_x(square_sum))], axis=1)
    small = links.sum_dp(small)
    loss = small[0, heads] / (width * valid_count)

    mixed = dot(result.astype(BF), chooser, 1, 1).astype(BF)
    high = lax.reduce_precision(grad_tokens, 8, 7)
    low = (grad_tokens - high).astype(BF)
    unplaced = dot(jnp.concatenate([high.astype(BF), low], axis=0), chooser, 1, 1)
    grad_tokens = unplaced[:rows] + unplaced[rows:]

    return (
        mixed,
        loss,
        grad_tokens,
        sum_attn[:, :hd],
        sum_attn[:, hd : 2 * hd],
        sum_attn[:, 2 * hd : 3 * hd],
        sum_attn[:, 3 * hd :].T,
        sum_gate,
        sum_up,
        sum_down,
        gains[0],
        gains[1],
        small[:, :heads],
    )


def solution(mesh):
    return jax.shard_map(
        local,
        mesh=mesh,
        in_specs=(
            P(("dp", "tensor"), None),
            P(("dp", "tensor"), None),
            P("dp"),
            P("dp"),
            P("dp"),
            P("dp"),
            P("dp", "tensor"),
            P("dp", "tensor"),
            P("dp", "tensor"),
            P("tensor", "dp"),
            P("dp", "tensor"),
            P("dp", "tensor"),
            P("tensor", "dp"),
            P("dp"),
            P("dp"),
            P(None, "tensor"),
        ),
        out_specs=(
            P(("dp", "tensor"), None),
            P(),
            P(("dp", "tensor"), None),
            P("dp", "tensor"),
            P("dp", "tensor"),
            P("dp", "tensor"),
            P("tensor", "dp"),
            P("dp", "tensor"),
            P("dp", "tensor"),
            P("tensor", "dp"),
            P("dp"),
            P("dp"),
            P(None, "tensor"),
        ),
        check_vma=False,
    )
```
